32 devices in a mesh: grp: 2 (over x), wide: 16 (over z, y, core).
Axes of the slice: x: 2, y: 2, z: 4, core: 2. Of those that a mesh axis runs over, the one named last changes fastest.
Arguments:
- voltages: bfloat16 [2048, 2, 8240], P(('grp', 'wide')), parts along dimension 0, may hold values from -6 to 6
- taps: float32 [4, 16], replicated, may hold values from -3 to 3
- flags: int32 [2048], P(('grp', 'wide')), parts along dimension 0, may hold values 0 or 1
- positions: float32 [2, 1024], replicated, may hold values from -20 to 20
- beam_index: int32 [512], P('grp'), parts along dimension 0, may hold values from 0 to 1023
Outputs:
- power: float32 [512, 16, 128], P(('grp', 'wide')), parts along dimension 0
The draws below stay inside these ranges and needn't reach their ends.
There are 2 independent parts, one for each index of `grp`. The reference program is written for one: setup_inputs(seed, part) draws one part's arguments, and reference() takes and returns one part's arrays. A program takes and returns all parts, laid end to end along the dimension named above; an argument that names none is the same for every part. Nothing has to cross between parts.
Inputs may be any that keep to these rules, and one draw needn't show every extreme that they name: 1 keeps an antenna, 0 flags it.
All inputs are finite; a program needn't handle non-finite values. No bound on the sum of `flags` on one device may be relied on, other than what follows from the above.
Results may differ from the reference program's by a relative error of at most 0.0075.
Values may be sent and summed in bfloat16 or wider, within the bound.
No kernel may reach another device: no remote copies, remote signals or barrier semaphores. Data moves between devices by JAX's collectives and lax.ppermute only.
A program may use at most 128 MiB of HBM per device.

```python
import math
import jax
import jax.numpy as jnp
from jax import lax

ANTENNAS = 1024
BEAMS = 256
TAPS = 4
ITERS = 2
SPECTRA = 512
CHANNELS = 16


def touch_ends(entries, rng, least, high):
    shape = entries.shape
    index_at = [jax.random.randint(jax.random.fold_in(rng, axis), (), 0, shape[axis]) for axis in range(len(shape))]
    entries = entries.at[tuple(index_at)].set(least)
    longest = shape.index(max(shape))
    index_at[longest] = (index_at[longest] + 1) % shape[longest]
    return entries.at[tuple(index_at)].set(high)


def shard_levels(stream_key, extent, split, low, top_value):
    def one(position, blocks):
        heights = jax.random.uniform(jax.random.fold_in(jax.random.fold_in(stream_key, 6), position), (blocks,), jnp.float32, low / len(split), top_value / len(split))
        return jnp.repeat(jnp.exp(heights), extent[position] // blocks).reshape((-1,) + (1,) * (len(extent) - position - 1))

    gain = one(*split[0])
    for cut in split[1:]:
        gain = gain * one(*cut)
    return gain


def normal_values(key, extent, deviation, bound, shards=(), held_as=jnp.bfloat16):
    values = deviation * jax.random.normal(key, extent, jnp.float32)
    if shards:
        values = values * shard_levels(key, extent, shards, -0.22, 0.18)
    return jnp.clip(values, -bound, bound).astype(held_as)


def setup_inputs(seed: int = 0, part: int = 0) -> dict:
    arg_keys = jax.random.split(jax.random.key(seed), 6)
    part_keys = jax.random.split(jax.random.fold_in(arg_keys[5], part), 6)
    return {
        "voltages": normal_values(part_keys[0], (ANTENNAS, 2, (SPECTRA + TAPS - 1) * CHANNELS), 1.0, 6.0, ((0, 16),)),
        "taps": normal_values(arg_keys[1], (TAPS, CHANNELS), TAPS ** -0.5, 3.0, (), jnp.float32),
        "flags": touch_ends((jax.random.randint(part_keys[2], (ANTENNAS,), 0, 8) < 7).astype(jnp.int32), jax.random.fold_in(part_keys[2], 1), 0, 1),
        "positions": jnp.clip(jax.random.uniform(arg_keys[3], (2, ANTENNAS), jnp.float32, -20.0, 20.0), -20.0, 20.0),
        "beam_index": touch_ends(jax.random.randint(part_keys[4], (BEAMS,), 0, 1024), jax.random.fold_in(part_keys[4], 1), 0, 1023).astype(jnp.int32),
    }


damping = 0.5
grid_side = 32

def channelize(voltages, taps, flags):
    count = voltages.shape[0]
    chans = taps.shape[1]
    ntaps = taps.shape[0]
    total = voltages.shape[2] // chans - ntaps + 1
    samples = voltages.astype(jnp.float32).reshape(count, 2, total + ntaps - 1, chans)
    filtered = taps[0][None, None, None, :] * samples[:, :, 0:total, :]
    for tap in range(1, ntaps):
        filtered = filtered + taps[tap][None, None, None, :] * samples[:, :, tap:tap + total, :]
    branch = jnp.arange(chans, dtype=jnp.int32)
    angle = 2.0 * math.pi / chans * (branch[:, None] * branch[None, :] % chans).astype(jnp.float32)
    cosine = jnp.cos(angle)
    sine = jnp.sin(angle)
    high = lax.Precision.HIGHEST
    real_in = filtered[:, 0]
    imag_in = filtered[:, 1]
    real_out = jnp.einsum('asp,pc->acs', real_in, cosine, precision=high) + jnp.einsum('asp,pc->acs', imag_in, sine, precision=high)
    imag_out = jnp.einsum('asp,pc->acs', imag_in, cosine, precision=high) - jnp.einsum('asp,pc->acs', real_in, sine, precision=high)
    keep = flags.astype(jnp.float32)[:, None, None] / math.sqrt(chans)
    return jnp.stack([real_out * keep, imag_out * keep]).astype(jnp.bfloat16)

def steering(channel, positions, beam_index, chans):
    column = (beam_index % grid_side).astype(jnp.float32)
    row_cell = (beam_index // grid_side).astype(jnp.float32)
    east = (column + 0.5) / grid_side - 0.5
    north = (row_cell + 0.5) / grid_side - 0.5
    ratio = 1.0 + 0.5 * channel.astype(jnp.float32) / chans
    phase = 2.0 * math.pi * ratio * (positions[0][:, None] * east[None, :] + positions[1][:, None] * north[None, :])
    return (jnp.cos(phase), -jnp.sin(phase))

def form_beams(blocks, channel, positions, beam_index, total, chans):
    high = lax.Precision.HIGHEST
    cov_real = 0.0
    cov_imag = 0.0
    for block in blocks:
        left = jnp.concatenate([block[0], block[1]], axis=1)
        turned = jnp.concatenate([block[1], -block[0]], axis=1)
        cov_real = cov_real + jnp.dot(left, left.T, preferred_element_type=jnp.float32)
        cov_imag = cov_imag + jnp.dot(turned, left.T, preferred_element_type=jnp.float32)
    cov_real = cov_real / total
    cov_imag = cov_imag / total
    count = cov_real.shape[0]
    diagonal = jnp.diagonal(cov_real)
    loading = jnp.mean(diagonal) + 1e-05
    scaling = (damping / (diagonal + loading))[:, None]
    steer_real, steer_imag = steering(channel, positions, beam_index, chans)
    weight_real = scaling * steer_real
    weight_imag = scaling * steer_imag
    for sweep in range(ITERS):
        image_real = jnp.dot(cov_real, weight_real, precision=high) - jnp.dot(cov_imag, weight_imag, precision=high) + loading * weight_real
        image_imag = jnp.dot(cov_real, weight_imag, precision=high) + jnp.dot(cov_imag, weight_real, precision=high) + loading * weight_imag
        weight_real = weight_real + scaling * (steer_real - image_real)
        weight_imag = weight_imag + scaling * (steer_imag - image_imag)
    low_real = weight_real.astype(jnp.bfloat16)
    low_imag = weight_imag.astype(jnp.bfloat16)
    plain = jnp.concatenate([low_real, low_imag], axis=0)
    mixed = jnp.concatenate([low_real, -low_imag], axis=0)
    contract = (((0,), (0,)), ((), ()))
    reals = []
    imags = []
    for block in blocks:
        reals.append(lax.dot_general(plain, jnp.concatenate([block[0], block[1]], axis=0), contract, preferred_element_type=jnp.float32))
        imags.append(lax.dot_general(mixed, jnp.concatenate([block[1], block[0]], axis=0), contract, preferred_element_type=jnp.float32))
    norm_factor = 1.0 / math.sqrt(count)
    beams = jnp.stack([jnp.concatenate(reals, axis=-1), jnp.concatenate(imags, axis=-1)]) * norm_factor
    return beams.astype(jnp.bfloat16)

def detect(beams):
    floats = beams.astype(jnp.float32)
    energy = floats[:, 0] * floats[:, 0] + floats[:, 1] * floats[:, 1]
    shape = energy.shape
    return energy.reshape(shape[0], shape[1], shape[2] // 4, 4).sum(axis=-1)

def reference(voltages, taps, flags, positions, beam_index):
    spectra = channelize(voltages, taps, flags)
    chans = taps.shape[1]
    total = spectra.shape[3]
    moved = jnp.moveaxis(spectra, 2, 0)

    def one_channel(operands):
        channel, block = operands
        return form_beams([block], channel, positions, beam_index, total, chans)
    beams = lax.map(one_channel, (jnp.arange(chans, dtype=jnp.int32), moved))
    return jnp.transpose(detect(beams), (1, 0, 2))
```

```python
import functools
import math

import jax
import jax.numpy as jnp
import numpy as np
from jax import lax
from jax.experimental import pallas as pl
from jax.experimental.pallas import tpu as pltpu
from jax.sharding import PartitionSpec as P

ITERS = 2

damping = 0.5
grid_side = 32
group = 4
LANES = 128
PACK = 16

NT = (((1,), (1,)), ((), ()))
NN = (((1,), (0,)), ((), ()))


def round_up(value, unit):
    return -(-value // unit) * unit


def dot(a, b, dims):
    return lax.dot_general(a, b, dims, preferred_element_type=jnp.float32)


def swap_pairs(x):
    lane = lax.broadcasted_iota(jnp.int32, x.shape, x.ndim - 1)
    width = x.shape[-1]
    after = pltpu.roll(x, width - 1, x.ndim - 1)
    before = pltpu.roll(x, 1, x.ndim - 1)
    return jnp.where(lane % 2 == 0, -after, before)


class Plan:
    def __init__(self, count, length, ntaps, chans):
        self.rows = 2 * count
        self.count = count
        self.chans = chans
        self.ntaps = ntaps
        self.total = length // chans - ntaps + 1
        self.block = max(LANES, chans)
        self.per = self.block // chans
        self.reach = self.block + (ntaps - 1) * chans
        self.window = round_up(self.reach, LANES)
        self.length = length
        self.step = PACK // self.per
        self.steps = self.total // PACK


def dft_tables(plan):
    row = np.arange(plan.chans * plan.per)
    chan = row // plan.per
    lane = np.arange(plan.window)
    angle = 2.0 * np.pi / plan.chans * ((chan[:, None] * (lane % plan.chans)[None, :]) % plan.chans)
    return np.cos(angle).astype(np.float32), np.sin(angle).astype(np.float32)


def channelize_kernel(plan, taps_ref, keep_ref, cos_ref, sin_ref, v_ref, o_ref, w_ref):
    n = plan.chans * plan.per
    row = lax.broadcasted_iota(jnp.int32, (n, plan.window), 0)
    lane = lax.broadcasted_iota(jnp.int32, (n, plan.window), 1)
    behind = lane // plan.chans - row % plan.per
    coef = jnp.zeros((n, plan.window), jnp.float32)
    for tap in range(plan.ntaps):
        coef = jnp.where(behind == tap, taps_ref[tap : tap + 1, :], coef)
    for part, table in enumerate((cos_ref, sin_ref)):
        full = coef * table[...]
        high = full.astype(jnp.bfloat16)
        w_ref[part * n : (part + 1) * n] = high
        w_ref[(2 + part) * n : (3 + part) * n] = (full - high.astype(jnp.float32)).astype(jnp.bfloat16)
    keep = jnp.concatenate([keep_ref[...]] * plan.step, axis=1)

    def emit(step, pieces):
        x = pieces[0] if len(pieces) == 1 else jnp.concatenate(pieces, axis=0)
        width = x.shape[1]
        d = dot(w_ref[:, :width], x, NT)
        d = d[: 2 * n] + d[2 * n :]
        out = (d[:n] - swap_pairs(d[n:])) * keep
        if plan.per * plan.step == PACK and plan.per == 8 and plan.rows == LANES:
            for chan in range(plan.chans):
                part = out[chan * plan.per : (chan + 1) * plan.per]
                both = jnp.concatenate([part[:, :LANES], part[:, LANES:]], axis=0)
                o_ref[chan, pl.ds(pl.multiple_of(step * PACK, PACK), PACK), :] = both.astype(jnp.bfloat16)
        else:
            o_ref[pl.ds(step, 1)] = out.astype(jnp.bfloat16)[None]

    def load(start, width):
        return v_ref[:, :, pl.ds(start, width)].reshape(plan.rows, width)

    def body(step, carry):
        base = pl.multiple_of(step * plan.step * plan.block, LANES)
        emit(step, [load(pl.multiple_of(base + i * plan.block, LANES), plan.window) for i in range(plan.step)])
        return carry

    lax.fori_loop(0, plan.steps - 1, body, 0)
    step = plan.steps - 1
    pieces = []
    for i in range(plan.step):
        start = (step * plan.step + i) * plan.block
        width = min(plan.window, plan.length - start)
        piece = load(start, width)
        if width < plan.window:
            fill = jnp.zeros((plan.rows, plan.window - width), piece.dtype)
            piece = jnp.concatenate([piece, fill], axis=1)
        pieces.append(piece)
    emit(step, pieces)


def channelize(voltages, taps, flags):
    count, _, length = voltages.shape
    ntaps, chans = taps.shape
    plan = Plan(count, length, ntaps, chans)
    keep = jnp.repeat(flags.astype(jnp.float32) / math.sqrt(chans), 2)[None, :]
    wide_taps = jnp.tile(taps, (1, plan.window // chans))
    cosine, sine = dft_tables(plan)
    direct = plan.per == 8 and plan.step == 2 and plan.rows == LANES
    n = plan.chans * plan.per
    if direct:
        shape = (chans, plan.total, plan.rows)
    else:
        shape = (plan.steps, n, plan.step * plan.rows)
    out = pl.pallas_call(
        functools.partial(channelize_kernel, plan),
        out_shape=jax.ShapeDtypeStruct(shape, jnp.bfloat16),
        scratch_shapes=[pltpu.VMEM((4 * n, plan.window), jnp.bfloat16)],
        name="channelize",
    )(wide_taps, keep, jnp.asarray(cosine), jnp.asarray(sine), voltages)
    if not direct:
        out = out.reshape(plan.steps, chans, plan.per, plan.step, plan.rows)
        out = out.transpose(1, 0, 3, 2, 4).reshape(chans, plan.total, plan.rows)
    return out


def steer_kernel(scale_ref, positions_ref, index_ref, o_ref):
    beams = index_ref.shape[1]
    row = lax.broadcasted_iota(jnp.int32, (beams, beams), 0)
    lane = lax.broadcasted_iota(jnp.int32, (beams, beams), 1)

    def column(line):
        return jnp.sum(jnp.where(row == lane, line, 0.0), axis=1, keepdims=True)

    index = index_ref[...]
    east = column((index % grid_side).astype(jnp.float32))
    north = column((index // grid_side).astype(jnp.float32))
    east = (east + 0.5) / grid_side - 0.5
    north = (north + 0.5) / grid_side - 0.5
    ratio = scale_ref[...]
    width = 2 * LANES

    def body(i, carry):
        where = pl.ds(pl.multiple_of(i * width, width), width)
        turns = ratio * (positions_ref[0:1, where] * east + positions_ref[1:2, where] * north)
        turns = turns - jnp.round(turns)
        odd = lax.broadcasted_iota(jnp.int32, turns.shape, 1) % 2
        turns = jnp.where(odd == 1, turns + 0.25, turns)
        turns = turns - jnp.round(turns)
        o_ref[:, where] = cos_turns(turns)
        return carry

    lax.fori_loop(0, positions_ref.shape[1] // width, body, 0)


def cos_turns(t):
    u = 0.25 - jnp.abs(t)
    s = u * u
    acc = jnp.full_like(s, SINE[-1])
    for c in SINE[-2::-1]:
        acc = acc * s + c
    return acc * u


SINE = [(-1) ** k * (2.0 * math.pi) ** (2 * k + 1) / math.factorial(2 * k + 1) for k in range(8)]


def steering(channel, positions, beam_index, chans):
    count = positions.shape[1]
    beams = beam_index.shape[0]
    ratio = (1.0 + 0.5 * channel.astype(jnp.float32) / chans).reshape(1, 1)
    return pl.pallas_call(
        steer_kernel,
        out_shape=jax.ShapeDtypeStruct((beams, 2 * count), jnp.float32),
        cost_estimate=pl.CostEstimate(flops=60 * beams * count, bytes_accessed=8 * beams * count, transcendentals=0),
        name="steer",
    )(ratio, jnp.repeat(positions, 2, axis=1), beam_index[None, :])


def solve_kernel(steer_ref, x_ref, o_ref, xx_ref, w_ref, low_ref, u_ref):
    sources, total, width = x_ref.shape
    lanes = sources * width
    count = lanes // 2
    beams = steer_ref.shape[0]

    squares = []
    for src in range(sources):
        where = slice(src * width, (src + 1) * width)

        def body(i, acc):
            at = pl.ds(pl.multiple_of(i * 64, 64), 64)
            x = x_ref[src, at, :]
            f = x.astype(jnp.float32)
            xx_ref[at, where] = x
            xx_ref[pl.ds(pl.multiple_of(total + i * 64, 64), 64), where] = swap_pairs(f).astype(jnp.bfloat16)
            return acc + jnp.sum((f * f).reshape(8, 8, width), axis=0)

        acc = lax.fori_loop(0, total // 64, body, jnp.zeros((8, width), jnp.float32))
        squares.append(jnp.sum(acc, axis=0, keepdims=True))
    square = jnp.concatenate(squares, axis=1)
    lane = lax.broadcasted_iota(jnp.int32, square.shape, 1)
    other = jnp.where(lane % 2 == 0, pltpu.roll(square, lanes - 1, 1), pltpu.roll(square, 1, 1))
    diagonal = (square + other) / total
    loading = jnp.sum(square, axis=1, keepdims=True) / (total * count) + 1e-05
    scaling = damping / (diagonal + loading)

    w = scaling * steer_ref[...]
    w_ref[...] = w
    low_ref[...] = w.astype(jnp.bfloat16)
    tile = 512

    def project():
        def body(i, carry):
            at = pl.ds(pl.multiple_of(i * tile, tile), tile)
            u_ref[:, at] = dot(low_ref[...], xx_ref[at, :], NT)
            return carry

        lax.fori_loop(0, 2 * total // tile, body, 0)

    for _ in range(ITERS):
        project()
        u_low = (u_ref[...] / total).astype(jnp.bfloat16)
        for i in range(lanes // tile):
            at = slice(i * tile, (i + 1) * tile)
            image = dot(u_low, xx_ref[:, at], NN)
            w = w_ref[:, at]
            w = w + scaling[:, at] * (steer_ref[:, at] - (image + loading * w))
            w_ref[:, at] = w
            low_ref[:, at] = w.astype(jnp.bfloat16)
    project()

    beam = (u_ref[...] * (1.0 / math.sqrt(count))).astype(jnp.bfloat16).astype(jnp.float32)
    square = beam * beam
    energy = square[:, :total] + square[:, total:]
    high = energy.astype(jnp.bfloat16)
    rest = (energy - high.astype(jnp.float32)).astype(jnp.bfloat16)
    row = lax.broadcasted_iota(jnp.int32, (total, total // group), 0)
    lane = lax.broadcasted_iota(jnp.int32, (total, total // group), 1)
    pick = jnp.where(row // group == lane, 1.0, 0.0).astype(jnp.bfloat16)
    o_ref[...] = (dot(high, pick, NN) + dot(rest, pick, NN)).astype(jnp.bfloat16)


def solve(steer, x):
    beams, lanes = steer.shape
    total = x.shape[1]
    return pl.pallas_call(
        solve_kernel,
        out_shape=jax.ShapeDtypeStruct((beams, total // group), jnp.bfloat16),
        scratch_shapes=[
            pltpu.VMEM((2 * total, lanes), jnp.bfloat16),
            pltpu.VMEM((beams, lanes), jnp.float32),
            pltpu.VMEM((beams, lanes), jnp.bfloat16),
            pltpu.VMEM((beams, 2 * total), jnp.float32),
        ],
        compiler_params=pltpu.CompilerParams(vmem_limit_bytes=40 * 2**20),
        name="solve",
    )(steer, x)


def local(voltages, taps, flags, positions, beam_index):
    chans = taps.shape[1]
    peers = lax.axis_size("wide")
    per_dev = chans // peers
    first = lax.axis_index("wide") * per_dev
    spectra = channelize(voltages, taps, flags)
    rows = spectra.shape[2]
    total = spectra.shape[1]
    moved = lax.all_to_all(spectra, "wide", split_axis=0, concat_axis=0, tiled=True)
    moved = moved.reshape(peers, per_dev, total, rows)
    spectra, positions, beam_index = lax.optimization_barrier((spectra, positions, beam_index))
    powers = []
    for offset in range(per_dev):
        steer = steering(first + offset, positions, beam_index, chans)
        x = moved[:, offset]
        if rows % LANES:
            x = x.transpose(1, 0, 2).reshape(1, total, peers * rows)
        powers.append(solve(steer, x))
    power = jnp.stack(powers)
    result = lax.all_to_all(power, "wide", split_axis=1, concat_axis=0, tiled=True)
    return jnp.transpose(result.astype(jnp.float32), (1, 0, 2))


def solution(mesh):
    in_specs = (P(("grp", "wide"), None, None), P(), P(("grp", "wide")), P(), P("grp"))
    out_specs = P(("grp", "wide"), None, None)
    return jax.shard_map(local, mesh=mesh, in_specs=in_specs, out_specs=out_specs, check_vma=False)
```

```python
import functools
import math

import jax
import jax.numpy as jnp
import numpy as np
from jax import lax
from jax.experimental import pallas as pl
from jax.experimental.pallas import tpu as pltpu
from jax.sharding import PartitionSpec as P

ITERS = 2

damping = 0.5
grid_side = 32
group = 4
LANES = 128
PACK = 16
PART = 128
CHUNKS = (1,)

NT = (((1,), (1,)), ((), ()))
NN = (((1,), (0,)), ((), ()))


def round_up(value, unit):
    return -(-value // unit) * unit


def dot(a, b, dims):
    return lax.dot_general(a, b, dims, preferred_element_type=jnp.float32)


def swap_pairs(x):
    lane = lax.broadcasted_iota(jnp.int32, x.shape, x.ndim - 1)
    width = x.shape[-1]
    after = pltpu.roll(x, width - 1, x.ndim - 1)
    before = pltpu.roll(x, 1, x.ndim - 1)
    return jnp.where(lane % 2 == 0, -after, before)


class Plan:
    def __init__(self, count, length, ntaps, chans):
        self.count = count
        self.rows = 2 * count
        self.chans = chans
        self.ntaps = ntaps
        self.total = length // chans - ntaps + 1
        self.block = max(LANES, chans)
        self.per = self.block // chans
        self.behind = (ntaps - 1) * chans
        self.window = round_up(self.block + self.behind, LANES)
        self.step = PACK // self.per
        self.part = math.gcd(self.total, PART)
        self.samples = self.part * chans
        self.next = min(
            width
            for width in range(LANES, self.samples + 1, LANES)
            if width >= self.behind and self.samples % width == 0
        )
        self.n = self.chans * self.per
        self.direct = self.per == 8 and self.rows == LANES


def filter_matrix(plan, taps_ref, w_ref):
    n = plan.n
    lane = lax.broadcasted_iota(jnp.int32, (8, plan.window), 1) % plan.chans
    tap_rows = []
    for tap in range(plan.ntaps):
        line = jnp.zeros((8, plan.window), jnp.float32)
        for branch in range(plan.chans):
            line = jnp.where(lane == branch, taps_ref[tap, branch], line)
        tap_rows.append(line[:1])
    row = lax.broadcasted_iota(jnp.int32, (n, plan.window), 0)
    lane = lax.broadcasted_iota(jnp.int32, (n, plan.window), 1)
    behind = lane // plan.chans - row % plan.per
    coef = jnp.zeros((n, plan.window), jnp.float32)
    for tap in range(plan.ntaps):
        coef = jnp.where(behind == tap, tap_rows[tap], coef)
    cycle = ((row // plan.per) * (lane % plan.chans)) % plan.chans
    turns = cycle.astype(jnp.float32) / plan.chans
    turns = turns - jnp.round(turns)
    for part, table in enumerate((cos_turns(turns), sin_turns(turns))):
        full = coef * table
        high = full.astype(jnp.bfloat16)
        w_ref[part * n : (part + 1) * n] = high
        w_ref[(2 + part) * n : (3 + part) * n] = (full - high.astype(jnp.float32)).astype(jnp.bfloat16)


def channelize_kernel(plan, taps_ref, flags_ref, v_ref, next_ref, o_ref, w_ref, keep_ref):
    n = plan.n

    @pl.when(pl.program_id(0) == 0)
    def _():
        filter_matrix(plan, taps_ref, w_ref)
        antenna = lax.broadcasted_iota(jnp.int32, (8, plan.rows), 1) // 2
        keep = jnp.zeros((8, plan.rows), jnp.float32)
        for index in range(plan.count):
            keep = jnp.where(antenna == index, flags_ref[index].astype(jnp.float32), keep)
        keep_ref[...] = keep / math.sqrt(plan.chans)

    keep = keep_ref[:1]
    lane = lax.broadcasted_iota(jnp.int32, (plan.rows, plan.next), 1)
    after = next_ref[...].reshape(plan.rows, plan.next)
    after = jnp.where(lane < plan.behind, after.astype(jnp.float32), 0.0).astype(jnp.bfloat16)

    def body(first, last):
        base = first * plan.step * plan.block
        need = plan.step * plan.block + plan.window - plan.block
        if last:
            x = v_ref[:, :, plan.samples - plan.step * plan.block :].reshape(plan.rows, plan.step * plan.block)
            x = jnp.concatenate([x, after[:, : need - plan.step * plan.block]], axis=1)
        else:
            x = v_ref[:, :, pl.ds(base, need)].reshape(plan.rows, need)
        x = jnp.concatenate([x[:, i * plan.block : i * plan.block + plan.window] for i in range(plan.step)], axis=0)
        d = dot(w_ref[...], x, NT)
        d = d[: 2 * n] + d[2 * n :]
        out = []
        for i in range(plan.step):
            at = slice(i * plan.rows, (i + 1) * plan.rows)
            out.append((d[:n, at] - swap_pairs(d[n:, at])) * keep)
        if plan.direct:
            for chan in range(plan.chans):
                at = slice(chan * plan.per, (chan + 1) * plan.per)
                both = jnp.concatenate([piece[at] for piece in out], axis=0)
                o_ref[chan, first * PACK : (first + 1) * PACK, :] = both.astype(jnp.bfloat16)
        else:
            o_ref[first] = jnp.concatenate(out, axis=1).astype(jnp.bfloat16)

    steps = plan.part // PACK
    for first in range(steps):
        body(first, first == steps - 1)


def channelize(voltages, taps, flags, first, parts):
    count, _, length = voltages.shape
    ntaps, chans = taps.shape
    plan = Plan(count, length, ntaps, chans)
    steps = plan.part // PACK
    ratio = plan.samples // plan.next
    if plan.direct:
        shape = (chans, parts * plan.part, plan.rows)
        out_spec = pl.BlockSpec((chans, plan.part, plan.rows), lambda i: (0, i, 0))
    else:
        shape = (parts * steps, plan.n, plan.step * plan.rows)
        out_spec = pl.BlockSpec((steps, plan.n, plan.step * plan.rows), lambda i: (i, 0, 0))
    samples = parts * plan.samples
    out = pl.pallas_call(
        functools.partial(channelize_kernel, plan),
        grid=(parts,),
        in_specs=[
            pl.BlockSpec(memory_space=pltpu.SMEM),
            pl.BlockSpec(memory_space=pltpu.SMEM),
            pl.BlockSpec((count, 2, plan.samples), lambda i: (0, 0, first + i)),
            pl.BlockSpec((count, 2, plan.next), lambda i: (0, 0, (first + i + 1) * ratio)),
        ],
        out_specs=out_spec,
        out_shape=jax.ShapeDtypeStruct(shape, jnp.bfloat16),
        scratch_shapes=[
            pltpu.VMEM((4 * plan.n, plan.window), jnp.bfloat16),
            pltpu.VMEM((8, plan.rows), jnp.float32),
        ],
        cost_estimate=pl.CostEstimate(
            flops=8 * plan.n * plan.window * plan.rows * samples // plan.block,
            bytes_accessed=8 * plan.rows * samples,
            transcendentals=0,
        ),
        name="channelize",
    )(taps, flags, voltages, voltages)
    if not plan.direct:
        out = out.reshape(parts * steps, chans, plan.per, plan.step, plan.rows)
        out = out.transpose(1, 0, 3, 2, 4).reshape(chans, parts * plan.part, plan.rows)
    return out


def steer_kernel(scale_ref, positions_ref, index_ref, o_ref):
    beams = index_ref.shape[1]
    row = lax.broadcasted_iota(jnp.int32, (beams, beams), 0)
    lane = lax.broadcasted_iota(jnp.int32, (beams, beams), 1)

    def column(line):
        return jnp.sum(jnp.where(row == lane, line, 0.0), axis=1, keepdims=True)

    index = index_ref[...]
    east = column((index % grid_side).astype(jnp.float32))
    north = column((index // grid_side).astype(jnp.float32))
    east = (east + 0.5) / grid_side - 0.5
    north = (north + 0.5) / grid_side - 0.5
    ratio = scale_ref[...]
    width = 2 * LANES

    def body(i, carry):
        where = pl.ds(pl.multiple_of(i * width, width), width)
        turns = ratio * (positions_ref[0:1, where] * east + positions_ref[1:2, where] * north)
        turns = turns - jnp.round(turns)
        odd = lax.broadcasted_iota(jnp.int32, turns.shape, 1) % 2
        turns = jnp.where(odd == 1, turns + 0.25, turns)
        turns = turns - jnp.round(turns)
        o_ref[:, where] = cos_turns(turns)
        return carry

    lax.fori_loop(0, positions_ref.shape[1] // width, body, 0)


def cos_turns(t):
    u = 0.25 - jnp.abs(t)
    s = u * u
    acc = jnp.full_like(s, SINE[-1])
    for c in SINE[-2::-1]:
        acc = acc * s + c
    return acc * u


def sin_turns(t):
    return jnp.where(t < 0, -1.0, 1.0) * cos_turns(jnp.abs(t) - 0.25)


SINE = [(-1) ** k * (2.0 * math.pi) ** (2 * k + 1) / math.factorial(2 * k + 1) for k in range(8)]


def steering(channel, positions, beam_index, chans):
    count = positions.shape[1]
    beams = beam_index.shape[0]
    ratio = (1.0 + 0.5 * channel.astype(jnp.float32) / chans).reshape(1, 1)
    return pl.pallas_call(
        steer_kernel,
        out_shape=jax.ShapeDtypeStruct((beams, 2 * count), jnp.float32),
        cost_estimate=pl.CostEstimate(flops=60 * beams * count, bytes_accessed=8 * beams * count, transcendentals=0),
        name="steer",
    )(ratio, jnp.repeat(positions, 2, axis=1), beam_index[None, :])


def solve_kernel(*refs):
    steer_hbm, *x_refs = refs[:-7]
    o_ref, xx_ref, steer_ref, w_ref, low_ref, u_ref, sem = refs[-7:]
    fetch = pltpu.make_async_copy(steer_hbm, steer_ref, sem)
    fetch.start()
    sources, _, width = x_refs[0].shape
    total = sum(x_ref.shape[1] for x_ref in x_refs)
    lanes = sources * width
    count = lanes // 2

    squares = []
    for src in range(sources):
        where = slice(src * width, (src + 1) * width)
        acc = jnp.zeros((8, width), jnp.float32)
        start = 0
        for x_ref in x_refs:
            size = math.gcd(x_ref.shape[1], 64)
            for i in range(0, x_ref.shape[1], size):
                x = x_ref[src, i : i + size, :]
                f = x.astype(jnp.float32)
                at = start + i
                xx_ref[at : at + size, where] = x
                xx_ref[total + at : total + at + size, where] = swap_pairs(f).astype(jnp.bfloat16)
                acc = acc + jnp.sum((f * f).reshape(size // 8, 8, width), axis=0)
            start += x_ref.shape[1]
        squares.append(jnp.sum(acc, axis=0, keepdims=True))
    square = jnp.concatenate(squares, axis=1)
    lane = lax.broadcasted_iota(jnp.int32, square.shape, 1)
    other = jnp.where(lane % 2 == 0, pltpu.roll(square, lanes - 1, 1), pltpu.roll(square, 1, 1))
    diagonal = (square + other) / total
    loading = jnp.sum(square, axis=1, keepdims=True) / (total * count) + 1e-05
    scaling = damping / (diagonal + loading)

    fetch.wait()
    w = scaling * steer_ref[...]
    w_ref[...] = w
    low_ref[...] = w.astype(jnp.bfloat16)
    tile = 512

    def project():
        def body(i, carry):
            at = pl.ds(pl.multiple_of(i * tile, tile), tile)
            u_ref[:, at] = dot(low_ref[...], xx_ref[at, :], NT)
            return carry

        lax.fori_loop(0, 2 * total // tile, body, 0)

    for _ in range(ITERS):
        project()
        u_low = (u_ref[...] / total).astype(jnp.bfloat16)
        for i in range(lanes // tile):
            at = slice(i * tile, (i + 1) * tile)
            image = dot(u_low, xx_ref[:, at], NN)
            w = w_ref[:, at]
            w = w + scaling[:, at] * (steer_ref[:, at] - (image + loading * w))
            w_ref[:, at] = w
            low_ref[:, at] = w.astype(jnp.bfloat16)
    project()

    beam = (u_ref[...] * (1.0 / math.sqrt(count))).astype(jnp.bfloat16).astype(jnp.float32)
    square = beam * beam
    energy = square[:, :total] + square[:, total:]
    high = energy.astype(jnp.bfloat16)
    rest = (energy - high.astype(jnp.float32)).astype(jnp.bfloat16)
    row = lax.broadcasted_iota(jnp.int32, (total, total // group), 0)
    lane = lax.broadcasted_iota(jnp.int32, (total, total // group), 1)
    pick = jnp.where(row // group == lane, 1.0, 0.0).astype(jnp.bfloat16)
    o_ref[...] = (dot(high, pick, NN) + dot(rest, pick, NN)).astype(jnp.bfloat16)


def solve(steer, xs):
    beams, lanes = steer.shape
    total = sum(x.shape[1] for x in xs)
    return pl.pallas_call(
        solve_kernel,
        in_specs=[pl.BlockSpec(memory_space=pl.ANY)] + [pl.BlockSpec(memory_space=pltpu.VMEM)] * len(xs),
        out_specs=pl.BlockSpec(memory_space=pltpu.VMEM),
        out_shape=jax.ShapeDtypeStruct((beams, total // group), jnp.bfloat16),
        scratch_shapes=[
            pltpu.VMEM((2 * total, lanes), jnp.bfloat16),
            pltpu.VMEM((beams, lanes), jnp.float32),
            pltpu.VMEM((beams, lanes), jnp.float32),
            pltpu.VMEM((beams, lanes), jnp.bfloat16),
            pltpu.VMEM((beams, 2 * total), jnp.float32),
            pltpu.SemaphoreType.DMA,
        ],
        compiler_params=pltpu.CompilerParams(vmem_limit_bytes=40 * 2**20),
        cost_estimate=pl.CostEstimate(flops=20 * beams * total * lanes, bytes_accessed=2**22, transcendentals=0),
        name="solve",
    )(steer, *xs)


def local(voltages, taps, flags, positions, beam_index):
    chans = taps.shape[1]
    peers = lax.axis_size("wide")
    per_dev = chans // peers
    first = lax.axis_index("wide") * per_dev
    plan = Plan(voltages.shape[0], voltages.shape[2], *taps.shape)
    parts = plan.total // plan.part
    sizes = [size * parts // sum(CHUNKS) for size in CHUNKS]
    moved = []
    start = 0
    for size in sizes:
        spectra = channelize(voltages, taps, flags, start, size)
        piece = lax.all_to_all(spectra, "wide", split_axis=0, concat_axis=0, tiled=True)
        moved.append(piece.reshape(peers, per_dev, size * plan.part, plan.rows))
        start += size
    spectra, positions, beam_index = lax.optimization_barrier((spectra, positions, beam_index))
    powers = []
    for offset in range(per_dev):
        steer = steering(first + offset, positions, beam_index, chans)
        xs = []
        for piece in moved:
            x = piece[:, offset]
            if plan.rows % LANES:
                x = x.transpose(1, 0, 2).reshape(1, x.shape[1], peers * plan.rows)
            xs.append(x)
        powers.append(solve(steer, xs))
    beams = beam_index.shape[0]
    power = jnp.stack(powers).reshape(per_dev, peers, beams // peers, -1).transpose(1, 0, 2, 3)
    result = lax.all_to_all(power, "wide", split_axis=0, concat_axis=0, tiled=True)
    result = result.reshape(chans, beams // peers, -1)
    return jnp.transpose(result.astype(jnp.float32), (1, 0, 2))


def solution(mesh):
    in_specs = (P(("grp", "wide"), None, None), P(), P(("grp", "wide")), P(), P("grp"))
    out_specs = P(("grp", "wide"), None, None)
    return jax.shard_map(local, mesh=mesh, in_specs=in_specs, out_specs=out_specs, check_vma=False)
```
